128 devices in a mesh: req: 4 (over z), seq: 32 (over x, y, core).
Axes of the slice: x: 4, y: 4, z: 4, core: 2. Of those that a mesh axis runs over, the one named last changes fastest.
Arguments:
- tokens: bfloat16 [4, 2048, 3584], P('req', 'seq'), may hold values from -6 to 6
- w_z: bfloat16 [3584, 7168], P('req', 'seq')
- w_x: bfloat16 [3584, 7168], P('req', 'seq'), may hold values from -0.09375 to 0.09375
- w_bc: bfloat16 [3584, 256], replicated, may hold values from -0.09375 to 0.09375
- w_dt: bfloat16 [3584, 112], replicated, may hold values from -0.09375 to 0.09375
- dt_bias: float32 [112], replicated, may hold values from -2 to 0
- a_rate: float32 [112], replicated, may hold values from 0.00024414062 to 0.2
- conv_weight: float32 [4, 7424], replicated, may hold values from -3 to 3
- conv_bias: float32 [7424], replicated, may hold values from -3 to 3
- d_skip: float32 [112], replicated, may hold values from 0.5 to 1.5
- norm_gain: float32 [7168], replicated, may hold values from 0.5 to 1.5
- lengths: int32 [4], P('req'), may hold values from 512 to 2048, as said below
Outputs:
- mixed: bfloat16 [4, 2048, 7168], P('req', 'seq')
The draws below stay inside these ranges and needn't reach their ends.
Inputs may be any that keep to these rules, and one draw needn't show every extreme that they name: `lengths`: each prompt has at least 512 valid positions, and the longest fills all 2048.
All inputs are finite; a program needn't handle non-finite values.
Results may differ from the reference program's by a relative error of at most 0.0055.
Values may be sent and summed in bfloat16 or wider, within the bound.
No kernel may reach another device: no remote copies, remote signals or barrier semaphores. Data moves between devices by JAX's collectives and lax.ppermute only.
A program may use at most 320 MiB of HBM per device.

```python
import math
import jax
import jax.numpy as jnp
from jax import lax

D = 3584
INNER = 7168
HEADS = 112
HEAD = 64
STATE = 64
GROUPS = 2
CONV = 4
TOK_DEV = 64
REQS = 4
LEN = 2048
XBC = 7424


def draw_lengths(key, part):
    first_key, second_key = jax.random.split(jax.random.fold_in(key, 11))
    drawn = jax.random.randint(first_key, (REQS,), LEN // 4, LEN + 1)
    longest = jax.random.randint(second_key, (), 0, REQS)
    return jnp.where(jnp.arange(REQS) == longest, LEN, drawn).astype(jnp.int32)


def draw_w_z(key, part):
    own_key = jax.random.fold_in(key, 5)
    group_width = INNER // GROUPS
    position = (jnp.arange(INNER) % group_width).astype(jnp.float32) / group_width
    base = jnp.clip(jax.random.normal(own_key, (D, INNER), jnp.float32), -6.0, 6.0)
    scale = 3.0 ** position
    return (base * scale[None, :] * D ** (-0.5)).astype(jnp.bfloat16)


def steps_of(rng, shape, cuts, low, largest):
    loudness, own = 1.0, jax.random.fold_in(rng, 6)
    for dim, parts in cuts:
        heights = jnp.exp(jax.random.uniform(jax.random.fold_in(own, dim), (parts,), jnp.float32, low / len(cuts), largest / len(cuts)))
        loudness = loudness * jnp.repeat(heights, shape[dim] // parts).reshape([-1 if axis == dim else 1 for axis in range(len(shape))])
    return loudness


def scatter_about(rng, extent, width, most, cuts=(), kind=jnp.bfloat16):
    array = width * jax.random.normal(rng, extent, jnp.float32)
    if cuts:
        array = array * steps_of(rng, extent, cuts, -0.22, 0.18)
    return jnp.clip(array, -most, most).astype(kind)


def setup_inputs(seed: int = 0) -> dict:
    arg_keys = jax.random.split(jax.random.key(seed), 13)
    return {
        "tokens": scatter_about(arg_keys[0], (REQS, LEN, D), 1.0, 6.0, ((0, 4), (1, 32))),
        "w_z": draw_w_z(jax.random.fold_in(arg_keys[12], 71), 0),
        "w_x": scatter_about(arg_keys[2], (D, INNER), D ** -0.5, 0.09375, ((0, 4), (1, 32))),
        "w_bc": scatter_about(arg_keys[3], (D, 2 * GROUPS * STATE), D ** -0.5, 0.09375),
        "w_dt": scatter_about(arg_keys[4], (D, HEADS), D ** -0.5, 0.09375),
        "dt_bias": jnp.clip(jax.random.uniform(arg_keys[5], (HEADS,), jnp.float32, -2.0, 0.0), -2.0, 0.0),
        "a_rate": jnp.clip(jnp.exp(jax.random.uniform(arg_keys[6], (HEADS,), jnp.float32, math.log(0.00024414062), math.log(0.2))), 0.00024414062, 0.2),
        "conv_weight": scatter_about(arg_keys[7], (CONV, XBC), CONV ** -0.5, 3.0, (), jnp.float32),
        "conv_bias": scatter_about(arg_keys[8], (XBC,), 0.5, 3.0, (), jnp.float32),
        "d_skip": jnp.clip(jax.random.uniform(arg_keys[9], (HEADS,), jnp.float32, 0.5, 1.5), 0.5, 1.5),
        "norm_gain": jnp.clip(1.0 + 0.1 * jax.random.normal(arg_keys[10], (INNER,), jnp.float32), 0.5, 1.5),
        "lengths": draw_lengths(jax.random.fold_in(arg_keys[12], 71), 0),
    }


PRECISE = lax.Precision.HIGHEST

def block_scan(x_heads, b_proj, c_proj, step_size, log_decay, state_in):
    per_group = x_heads.shape[1] // b_proj.shape[1]
    block_len = x_heads.shape[0]
    running = jnp.cumsum(log_decay, axis=0)
    causal_mask = jnp.arange(block_len)[:, None] >= jnp.arange(block_len)[None, :]
    gaps = running.T[:, :, None] - running.T[:, None, :]
    decay_mask = jnp.where(causal_mask[None], jnp.exp(jnp.minimum(gaps, 0.0)), 0.0)
    affinity = jnp.einsum('ign,jgn->gij', c_proj, b_proj, precision=PRECISE)
    mixing = decay_mask * jnp.repeat(affinity, per_group, axis=0) * step_size.T[:, None, :]
    intra_out = jnp.einsum('hij,jhp->ihp', mixing, x_heads, precision=PRECISE)
    c_heads = jnp.repeat(c_proj, per_group, axis=1)
    b_heads = jnp.repeat(b_proj, per_group, axis=1)
    carried = jnp.exp(running)[:, :, None] * jnp.einsum('ihn,hpn->ihp', c_heads, state_in, precision=PRECISE)
    tail_weight = jnp.exp(running[-1][None, :] - running) * step_size
    block_state = jnp.einsum('jhp,jhn->hpn', x_heads * tail_weight[:, :, None], b_heads, precision=PRECISE)
    return (intra_out + carried, block_state, running[-1])

def reference(tokens, w_z, w_x, w_bc, w_dt, dt_bias, a_rate, conv_weight, conv_bias, d_skip, norm_gain, lengths):

    def one_prompt(operands):
        prompt_tokens, length = operands
        gate_in = jnp.dot(prompt_tokens, w_z, preferred_element_type=jnp.float32).astype(jnp.bfloat16)
        x_in = jnp.dot(prompt_tokens, w_x, preferred_element_type=jnp.float32).astype(jnp.bfloat16)
        bc_proj = jnp.dot(prompt_tokens, w_bc, preferred_element_type=jnp.float32).astype(jnp.bfloat16)
        dt_raw = jnp.dot(prompt_tokens, w_dt, preferred_element_type=jnp.float32).astype(jnp.bfloat16)
        xbc = jnp.concatenate([x_in, bc_proj], axis=1)
        padded = jnp.pad(xbc.astype(jnp.float32), ((CONV - 1, 0), (0, 0)))
        conv_sum = conv_bias[None, :] + jnp.zeros((LEN, XBC), jnp.float32)
        for offset in range(CONV):
            conv_sum = conv_sum + conv_weight[offset][None, :] * padded[offset:offset + LEN]
        conved = lax.optimization_barrier(jax.nn.silu(conv_sum).astype(jnp.bfloat16)).astype(jnp.float32)
        x_heads = conved[:, :INNER].reshape(LEN, HEADS, HEAD)
        b_proj = conved[:, INNER:INNER + GROUPS * STATE].reshape(LEN, GROUPS, STATE)
        c_proj = conved[:, INNER + GROUPS * STATE:].reshape(LEN, GROUPS, STATE)
        step_size = jax.nn.softplus(dt_raw.astype(jnp.float32) + dt_bias[None, :])
        log_decay = -step_size * a_rate[None, :]
        blocks = LEN // TOK_DEV

        def advance(state_in, pieces):
            x_block, b_block, c_block, size_block, decay_block = pieces
            result, block_state, total_log = block_scan(x_block, b_block, c_block, size_block, decay_block, state_in)
            return (jnp.exp(total_log)[:, None, None] * state_in + block_state, result)
        final_state, results = lax.scan(advance, jnp.zeros((HEADS, HEAD, STATE), jnp.float32), (x_heads.reshape(blocks, TOK_DEV, HEADS, HEAD), b_proj.reshape(blocks, TOK_DEV, GROUPS, STATE), c_proj.reshape(blocks, TOK_DEV, GROUPS, STATE), step_size.reshape(blocks, TOK_DEV, HEADS), log_decay.reshape(blocks, TOK_DEV, HEADS)))
        result = results.reshape(LEN, HEADS, HEAD) + d_skip[None, :, None] * x_heads
        gated = result.reshape(LEN, INNER) * jax.nn.silu(gate_in.astype(jnp.float32))
        grouped = gated.reshape(LEN, GROUPS, INNER // GROUPS)
        inv_scale = lax.rsqrt(lax.optimization_barrier(jnp.mean(grouped * grouped, axis=2, keepdims=True)) + 1e-05)
        normed = (grouped * inv_scale).reshape(LEN, INNER) * norm_gain[None, :]
        valid_rows = jnp.arange(LEN, dtype=jnp.int32) < length
        return jnp.where(valid_rows[:, None], normed, 0.0).astype(jnp.bfloat16)
    return lax.map(one_prompt, (tokens, lengths))
```

```python
import functools

import jax
import jax.numpy as jnp
from jax import lax
from jax.experimental import pallas as pl
from jax.experimental.pallas import tpu as pltpu
from jax.sharding import PartitionSpec as P

STATE = 64
GROUPS = 2
HEAD = 64
CHUNK = 128
ROWS = 512
LANES = 128

F32 = jnp.float32
BF16 = jnp.bfloat16
NT = (((1,), (1,)), ((), ()))
NN = (((1,), (0,)), ((), ()))
TN = (((0,), (0,)), ((), ()))


def mm(a, b, dims):
    return lax.dot_general(a, b, dims, preferred_element_type=F32)


def halves(v):
    high = v.astype(BF16)
    return high, (v - high.astype(F32)).astype(BF16)


def silu(v):
    return v / (1.0 + jnp.exp(-v))


def mixer_kernel(
    shift_ref,
    tok_ref,
    w_ref,
    rest_ref,
    convx_ref,
    convr_ref,
    bias_ref,
    rate_ref,
    skip_ref,
    out_ref,
    state,
    z_buf,
    x_buf,
    r_buf,
    dt_buf,
):
    width = out_ref.shape[1]
    rows = tok_ref.shape[0]
    parts, _, depth = w_ref.shape
    half = 2 * STATE

    @pl.when(pl.program_id(0) == 0)
    def _():
        state[...] = jnp.zeros_like(state)
        x_buf[0:8] = jnp.zeros((8, width), F32)
        r_buf[0:8] = jnp.zeros((8, half), F32)

    z, x, rest = (0.0, 0.0, 0.0)
    for k in range(parts):
        t = tok_ref[:, k * depth : (k + 1) * depth]
        z = z + mm(t, w_ref[k, 0:width], NT)
        x = x + mm(t, w_ref[k, width : 2 * width], NT)
        rest = rest + mm(t, rest_ref[:, k * depth : (k + 1) * depth], NT)
    z_buf[...] = z.astype(BF16).astype(F32)
    x_buf[8 : 8 + rows] = x.astype(BF16).astype(F32)
    rest = rest.astype(BF16).astype(F32)
    r_buf[8 : 8 + rows] = rest[:, :half]
    dt_buf[...] = rest[:, half:]

    row = lax.broadcasted_iota(jnp.int32, (CHUNK, CHUNK), 0)
    col = lax.broadcasted_iota(jnp.int32, (CHUNK, CHUNK), 1)
    causal = row >= col
    tril = jnp.where(causal, 1.0, 0.0).astype(F32)
    lane_head = (lax.broadcasted_iota(jnp.int32, (1, width), 1) + shift_ref[0]) // HEAD

    def conv(window, taps_ref):
        total = taps_ref[4:5, :]
        for k in range(4):
            total = total + taps_ref[k : k + 1, :] * window[5 + k : 5 + k + CHUNK]
        return silu(total).astype(BF16)

    def spread(columns):
        out = columns[:, 0:1]
        for h in range(1, 4):
            out = jnp.where(lane_head == h, columns[:, h : h + 1], out)
        return out

    def step(c, carry):
        start = pl.multiple_of(c * CHUNK, CHUNK)
        xb = conv(x_buf[pl.ds(start, CHUNK + 8), :], convx_ref)
        bc = conv(r_buf[pl.ds(start, CHUNK + 8), :], convr_ref).astype(F32)
        b = bc[:, :STATE].astype(BF16)
        c_ = bc[:, STATE:].astype(BF16)
        xf = xb.astype(F32)
        pre = dt_buf[pl.ds(start, CHUNK), :] + bias_ref[...]
        size = jnp.maximum(pre, 0.0) + jnp.log1p(jnp.exp(-jnp.abs(pre)))
        decay = -size * rate_ref[...]
        running = lax.dot_general(
            tril, decay, NN, precision=lax.Precision.HIGHEST, preferred_element_type=F32
        )
        run_t = jnp.transpose(running)
        size_t = jnp.transpose(size)
        affinity = jnp.where(causal, mm(c_, b, NT), 0.0)
        intra = jnp.zeros((CHUNK, width), F32)
        for h in range(4):
            gap = running[:, h : h + 1] - run_t[h : h + 1, :]
            mix = affinity * jnp.exp(jnp.minimum(gap, 0.0)) * size_t[h : h + 1, :]
            high, low = halves(mix)
            own = jnp.where(lane_head == h, xf, 0.0).astype(BF16)
            intra = intra + mm(high, own, NN) + mm(low, own, NN)
        run_wide = spread(running)
        size_wide = spread(size)
        last = run_wide[CHUNK - 1 : CHUNK, :]
        old = state[...]
        high, low = halves(old)
        carried = jnp.exp(run_wide) * (mm(c_, high, NN) + mm(c_, low, NN))
        high, low = halves(xf * (jnp.exp(last - run_wide) * size_wide))
        state[...] = jnp.exp(last) * old + (mm(b, high, TN) + mm(b, low, TN))
        result = intra + carried + skip_ref[...] * xf
        gated = result * silu(z_buf[pl.ds(start, CHUNK), :])
        out_ref[pl.ds(start, CHUNK), :] = gated.astype(BF16)
        return carry

    lax.fori_loop(0, rows // CHUNK, step, 0)
    x_buf[0:8] = x_buf[rows : rows + 8]
    r_buf[0:8] = r_buf[rows : rows + 8]


def norm_kernel(valid_ref, in_ref, gain_ref, out_ref):
    pieces, rows, width = in_ref.shape
    per = pieces // GROUPS
    keep = lax.broadcasted_iota(jnp.int32, (rows, 1), 0) < valid_ref[0]
    for g in range(GROUPS):
        total = jnp.zeros((rows, width), F32)
        for d in range(per):
            v = in_ref[g * per + d].astype(F32)
            total = total + v * v
        mean = jnp.sum(total, axis=1, keepdims=True) / (per * width)
        scale = lax.rsqrt(mean + 1e-05)
        for d in range(g * per, (g + 1) * per):
            v = in_ref[d].astype(F32) * scale * gain_ref[d : d + 1, :]
            out_ref[:, d * width : (d + 1) * width] = jnp.where(keep, v, 0.0).astype(BF16)


def mixer(tokens, weights, rest, convx, convr, bias, rate, skip, shift):
    length, d_model = tokens.shape
    width = skip.shape[1]
    whole = lambda a: pl.BlockSpec(
        a.shape, lambda i: (0,) * a.ndim, pipeline_mode=pl.Buffered(1)
    )
    return pl.pallas_call(
        mixer_kernel,
        grid=(length // ROWS,),
        in_specs=[
            pl.BlockSpec(memory_space=pltpu.SMEM),
            pl.BlockSpec((ROWS, d_model), lambda i: (i, 0)),
            whole(weights),
            whole(rest),
            whole(convx),
            whole(convr),
            whole(bias),
            whole(rate),
            whole(skip),
        ],
        out_specs=pl.BlockSpec((ROWS, width), lambda i: (i, 0)),
        out_shape=jax.ShapeDtypeStruct((length, width), BF16),
        scratch_shapes=[
            pltpu.VMEM((STATE, width), F32),
            pltpu.VMEM((ROWS, width), F32),
            pltpu.VMEM((ROWS + 8, width), F32),
            pltpu.VMEM((ROWS + 8, 2 * STATE), F32),
            pltpu.VMEM((ROWS, LANES), F32),
        ],
        compiler_params=pltpu.CompilerParams(vmem_limit_bytes=48 * 1024 * 1024),
        name="mixer",
    )(shift, tokens, weights, rest, convx, convr, bias, rate, skip)


def local(
    tokens,
    w_z,
    w_x,
    w_bc,
    w_dt,
    dt_bias,
    a_rate,
    conv_weight,
    conv_bias,
    d_skip,
    norm_gain,
    lengths,
):
    own_rows = tokens[0]
    num_rows, d_model = own_rows.shape
    width = w_z.shape[1]
    seq = lax.axis_size("seq")
    me = lax.axis_index("seq")
    inner = width * seq

    both = jnp.concatenate([w_z.T, w_x.T], axis=0)
    weights = lax.all_gather(both, "req", axis=0)
    everyone = lax.all_gather(own_rows, "seq", axis=0, tiled=True)

    first = me * width
    head = first // HEAD
    group = me * GROUPS // seq
    cut = lambda a, at, n: lax.dynamic_slice_in_dim(a, at, n, axis=a.ndim - 1)
    pick = lambda a: jnp.concatenate(
        [cut(a, group * STATE, STATE), cut(a, (GROUPS + group) * STATE, STATE)], axis=-1
    )
    dt_rows = lax.dynamic_slice_in_dim(w_dt.T, head, 4, axis=0)
    rest = jnp.concatenate(
        [pick(w_bc).T, dt_rows, jnp.zeros((LANES - 4, d_model), BF16)], axis=0
    )
    taps = jnp.concatenate([conv_weight, conv_bias[None]], axis=0)
    convx = cut(taps, first, width)
    convr = pick(taps[:, inner:])
    pad = lambda a: jnp.pad(cut(a, head, 4), (0, LANES - 4))[None]
    shift = first - head * HEAD
    skip = cut(jnp.repeat(d_skip, HEAD), first, width)[None]
    gated = mixer(
        everyone, weights, rest, convx, convr, pad(dt_bias), pad(a_rate), skip, shift[None]
    )
    pieces = lax.all_to_all(
        gated.reshape(seq, num_rows, width), "seq", split_axis=0, concat_axis=0, tiled=True
    )
    valid = lengths - me * num_rows
    mixed = pl.pallas_call(
        norm_kernel,
        in_specs=[
            pl.BlockSpec(memory_space=pltpu.SMEM),
            pl.BlockSpec(memory_space=pltpu.VMEM),
            pl.BlockSpec(memory_space=pltpu.VMEM),
        ],
        out_specs=pl.BlockSpec(memory_space=pltpu.VMEM),
        out_shape=jax.ShapeDtypeStruct((num_rows, inner), BF16),
        name="norm",
    )(valid, pieces, norm_gain.reshape(seq, width))
    return mixed[None]


def solution(mesh):
    placed = (
        P("req", "seq", None),
        P("req", "seq"),
        P("req", "seq"),
        P(),
        P(),
        P(),
        P(),
        P(),
        P(),
        P(),
        P(),
        P("req"),
    )
    return jax.shard_map(
        local, mesh=mesh, in_specs=placed, out_specs=P("req", "seq", None), check_vma=False
    )
```
